256 devices in a mesh: ctx: 128 (over z, y_lo, x, core), head: 2 (over y_hi).
Axes of the slice: x: 4, y: 4 (y_hi: 2, y_lo: 2; y = y_hi * 2 + y_lo), z: 8, core: 2. Of those that a mesh axis runs over, the one named last changes fastest.
Arguments:
- queries: bfloat16 [49152, 2048], P('ctx', 'head')
- keys: bfloat16 [49152, 512], P('ctx', 'head')
- values: bfloat16 [49152, 512], P('ctx', 'head'), may hold values from -6 to 6
- block_start: int32 [384], P('ctx'), may hold values from 0 to 49024, as said below
- out_weight: bfloat16 [2048, 4096], P('head'), may hold values from -0.125 to 0.125
Outputs:
- attended: bfloat16 [49152, 4096], P('ctx', 'head')
The draws below stay inside these ranges and needn't reach their ends.
Inputs may be any that keep to these rules, and one draw needn't show every extreme that they name: block_start never falls; every document is a whole number of blocks and at most 3072 tokens long, and one document is exactly 3072 tokens long; the first and the last block each begin a document.
All inputs are finite; a program needn't handle non-finite values.
Results may differ from the reference program's by a relative error of at most 0.012.
Values may be sent and summed in bfloat16 or wider, within the bound.
A program may use at most 64 MiB of HBM per device.

```python
import jax
import jax.numpy as jnp
from jax import lax

D = 4096
QUERY_HEADS = 16
KEY_VALUE_HEADS = 4
HEAD_SIZE = 128
BLOCK = 128
SPAN = 8
SHARD_TOKENS = 384
CONTEXT_TOKENS = 49152
MAXDOC = 3072
N_CTX = 128
N_HEAD = 2


def shared_pair(key):
    key_sample = jnp.clip(jax.random.normal(jax.random.fold_in(key, 12), (CONTEXT_TOKENS, KEY_VALUE_HEADS, HEAD_SIZE), jnp.float32), -4.0, 4.0)
    query_sample = jnp.clip(jax.random.normal(jax.random.fold_in(key, 11), (CONTEXT_TOKENS, QUERY_HEADS, HEAD_SIZE), jnp.float32), -4.0, 4.0)
    return (query_sample.reshape(CONTEXT_TOKENS, QUERY_HEADS * HEAD_SIZE), key_sample.reshape(CONTEXT_TOKENS, KEY_VALUE_HEADS * HEAD_SIZE))


def draw_queries(key, part):
    return shared_pair(key)[0].astype(jnp.bfloat16)


def draw_keys(key, part):
    return shared_pair(key)[1].astype(jnp.bfloat16)


def draw_block_start(key, part):
    blocks = CONTEXT_TOKENS // BLOCK
    longest = MAXDOC // BLOCK
    lens = jax.random.randint(jax.random.fold_in(key, 21), (blocks,), 1, longest + 1)
    lens = jnp.where(jnp.arange(blocks) == 0, longest, lens).astype(jnp.int32)
    ends = jnp.cumsum(lens)
    begins = ends - lens
    slots = jnp.where(begins < blocks, begins, blocks)
    marks = jnp.zeros((blocks,), jnp.int32).at[slots].set(1, mode='drop')
    marks = marks.at[blocks - 1].set(1)
    firsts = lax.cummax(jnp.arange(blocks, dtype=jnp.int32) * marks, axis=0)
    return (firsts * BLOCK).astype(jnp.int32)


def levels(key, shape, shards, low, high):
    def one(dim, parts):
        heights = jax.random.uniform(jax.random.fold_in(jax.random.fold_in(key, 6), dim), (parts,), jnp.float32, low / len(shards), high / len(shards))
        return jnp.repeat(jnp.exp(heights), shape[dim] // parts).reshape((-1,) + (1,) * (len(shape) - dim - 1))

    factor_of = one(*shards[0])
    for cut in shards[1:]:
        factor_of = factor_of * one(*cut)
    return factor_of


def bell_draw(rng, shape, width, most, cuts=(), held_as=jnp.bfloat16):
    factor_of = levels(rng, shape, cuts, -0.22, 0.18) if cuts else 1.0
    entries = jax.random.normal(rng, shape, jnp.float32) * width * factor_of
    return jnp.minimum(jnp.maximum(entries, -most), most).astype(held_as)


def setup_inputs(seed: int = 0) -> dict:
    streams_of = jax.random.split(jax.random.key(seed), 6)
    return {
        "queries": draw_queries(jax.random.fold_in(streams_of[5], 71), 0),
        "keys": draw_keys(jax.random.fold_in(streams_of[5], 71), 0),
        "values": bell_draw(streams_of[2], (CONTEXT_TOKENS, KEY_VALUE_HEADS * HEAD_SIZE), 1.0, 6.0, ((0, 128), (1, 2))),
        "block_start": draw_block_start(jax.random.fold_in(streams_of[5], 71), 0),
        "out_weight": bell_draw(streams_of[4], (QUERY_HEADS * HEAD_SIZE, D), (QUERY_HEADS * HEAD_SIZE) ** -0.5, 0.125, ((0, 2),)),
    }


def reference(queries, keys, values, block_start, out_weight):
    query_group = QUERY_HEADS // KEY_VALUE_HEADS
    padding = SPAN * SHARD_TOKENS
    window_width = padding + SHARD_TOKENS
    scale = HEAD_SIZE ** -0.5
    padded_keys = jnp.concatenate([jnp.zeros((padding, KEY_VALUE_HEADS * HEAD_SIZE), jnp.bfloat16), keys], axis=0)
    padded_values = jnp.concatenate([jnp.zeros((padding, KEY_VALUE_HEADS * HEAD_SIZE), jnp.bfloat16), values], axis=0)
    starts = jnp.repeat(block_start, BLOCK)

    def shard(index):
        first_token = index * SHARD_TOKENS
        query_rows = lax.dynamic_slice_in_dim(queries, first_token, SHARD_TOKENS, 0).astype(jnp.float32).reshape(SHARD_TOKENS, KEY_VALUE_HEADS, query_group, HEAD_SIZE)
        key_window = lax.dynamic_slice_in_dim(padded_keys, first_token, window_width, 0).astype(jnp.float32).reshape(window_width, KEY_VALUE_HEADS, HEAD_SIZE)
        value_window = lax.dynamic_slice_in_dim(padded_values, first_token, window_width, 0).astype(jnp.float32).reshape(window_width, KEY_VALUE_HEADS, HEAD_SIZE)
        scores = jnp.einsum("pgcd,jgd->gcpj", query_rows, key_window) * scale
        q_pos = first_token + jnp.arange(SHARD_TOKENS, dtype=jnp.int32)
        k_pos = first_token - padding + jnp.arange(window_width, dtype=jnp.int32)
        st = lax.dynamic_slice_in_dim(starts, first_token, SHARD_TOKENS, 0)
        valid = (k_pos[None, :] >= st[:, None]) & (k_pos[None, :] <= q_pos[:, None])
        masked = jnp.where(valid, scores, -1e30)
        top = jnp.max(masked, axis=-1, keepdims=True)
        expw = jnp.where(valid, jnp.exp(masked - top), 0.0)
        total = jnp.sum(expw, axis=-1)
        weights = lax.optimization_barrier(expw.astype(jnp.bfloat16)).astype(jnp.float32)
        numer = jnp.einsum("gcpj,jgd->gcpd", weights, value_window)
        out = (numer / total[..., None]).astype(jnp.bfloat16)
        return jnp.transpose(out, (2, 0, 1, 3)).reshape(SHARD_TOKENS, QUERY_HEADS * HEAD_SIZE)

    heads_out = lax.map(shard, jnp.arange(N_CTX, dtype=jnp.int32)).reshape(CONTEXT_TOKENS, QUERY_HEADS * HEAD_SIZE)
    half = QUERY_HEADS * HEAD_SIZE // N_HEAD
    summed = jnp.zeros((CONTEXT_TOKENS, D), jnp.float32)
    for part in range(N_HEAD):
        partial_value = jnp.dot(heads_out[:, part * half:(part + 1) * half], out_weight[part * half:(part + 1) * half], preferred_element_type=jnp.float32)
        summed = summed + lax.optimization_barrier(partial_value.astype(jnp.bfloat16)).astype(jnp.float32)
    return summed.astype(jnp.bfloat16)
```

```python
import math

import jax
import jax.numpy as jnp
from jax import lax
from jax.experimental import pallas as pl
from jax.experimental.pallas import tpu as pltpu
from jax.sharding import PartitionSpec as P

HEAD_SIZE = 128
BLOCK = 128
SPAN = 8
NX = 4
NY = 2
ROW = NX * 2
PLANE = NY * ROW
MESH = pl.DeviceIdType.MESH
MASKED = -1e30


def span_of(n, size):
    start = n * size
    return pl.ds(start if isinstance(start, int) else pl.multiple_of(start, size), size)


def kernel(
    starts,
    q_hbm,
    k_hbm,
    v_hbm,
    w_hbm,
    o_hbm,
    qb,
    kb,
    vb,
    sb,
    pb,
    bias,
    ho,
    hin,
    relay,
    wown,
    wfar,
    acc,
    outb,
    loc_sem,
    kv_send,
    kv_recv,
    w_send,
    w_recv,
    h_send,
    h_recv,
    f_send,
    f_recv,
    out_sem,
):
    n_ctx = lax.axis_size("ctx")
    tok = q_hbm.shape[0]
    kv_heads = k_hbm.shape[1] // HEAD_SIZE
    q_heads = q_hbm.shape[1] // HEAD_SIZE
    group = q_heads // kv_heads
    half = outb.shape[1]
    nz = n_ctx // PLANE
    piece = wfar.shape[0] // (nz * 2)
    up_hops = (nz - 1) // 2
    down_hops = nz - 1 - up_hops
    blocks = tok // BLOCK
    first = BLOCK
    keys = SPAN * tok + tok - first

    i = lax.axis_index("ctx")
    h = lax.axis_index("head")
    k = i % 2
    x = (i // 2) % NX
    y_lo = (i // ROW) % NY
    z = i // PLANE
    row0 = i - x * 2

    def dev(c, g):
        return {"ctx": c, "head": g}

    sib = dev(i + 1 - 2 * k, h)
    x_up = dev(row0 + ((x + 1) % NX) * 2, h)
    x_dn = dev(row0 + ((x + NX - 1) % NX) * 2, h)
    nxt = dev((i + ROW) % n_ctx, h)
    prv = dev((i + n_ctx - ROW) % n_ctx, h)
    yx = i + ROW - 2 * ROW * y_lo
    y_same = dev(yx, h)
    y_far = dev(yx, 1 - h)
    z_up = dev((i + PLANE) % n_ctx, h)
    z_dn = dev((i + n_ctx - PLANE) % n_ctx, h)

    local = []

    def load(src, dst):
        c = pltpu.make_async_copy(src, dst, loc_sem.at[len(local)])
        c.start()
        local.append(c)
        return c

    own = pl.ds(SPAN * tok, tok)
    kv_local = []
    for g in range(kv_heads):
        cols = pl.ds(g * HEAD_SIZE, HEAD_SIZE)
        kv_local.append(load(k_hbm.at[:, cols], kb.at[g, own, :]))
        kv_local.append(load(v_hbm.at[:, cols], vb.at[g, own, pl.ds(0, HEAD_SIZE)]))
    q_local = [load(q_hbm.at[:, pl.ds(n * HEAD_SIZE, HEAD_SIZE)], qb.at[n]) for n in range(q_heads)]
    w_local = load(w_hbm.at[:, span_of(h, half)], wown)

    barrier = pltpu.get_barrier_semaphore()
    partners = (sib, x_up, x_dn, nxt, prv, y_far, z_up, z_dn)
    for d in partners:
        pl.semaphore_signal(barrier, inc=1, device_id=d, device_id_type=MESH)
    pl.semaphore_wait(barrier, len(partners))

    def w_rows(p):
        return span_of(p, piece)

    def w_copy(p, slot, target):
        return pltpu.make_async_remote_copy(
            src_ref=wfar.at[w_rows(p), :],
            dst_ref=wfar.at[w_rows(p), :],
            send_sem=w_send.at[slot],
            recv_sem=w_recv.at[p],
            device_id=target,
            device_id_type=MESH,
        )

    mine = z * 2 + k
    w_first = pltpu.make_async_remote_copy(
        src_ref=w_hbm.at[w_rows(mine), span_of(1 - h, half)],
        dst_ref=wfar.at[w_rows(mine), :],
        send_sem=w_send.at[0],
        recv_sem=w_recv.at[mine],
        device_id=y_far,
        device_id_type=MESH,
    )
    w_first.start()

    w_plan = {0: [(mine, [(1, z_up), (2, z_dn), (3, sib)])]}
    slots = 4
    for d in range(1, down_hops + 1):
        w_plan[d] = []
        for reach, source, onward in (
            (up_hops, (z + nz - d) % nz, z_up),
            (down_hops, (z + d) % nz, z_dn),
        ):
            if d <= reach:
                targets = [onward, sib] if d < reach else [sib]
                w_plan[d].append((source * 2 + k, [(slots + n, c) for n, c in enumerate(targets)]))
                slots += len(targets)

    def w_step(d):
        for p, sends in w_plan[d]:
            w_copy(p, 0, sib).wait_recv()
            for slot, target in sends:
                w_copy(p, slot, target).start()

    def w_rest():
        for other in range(nz):
            w_copy(other * 2 + 1 - k, 0, sib).wait_recv()

    def view(g, t, pos):
        rows = span_of(pos, tok)
        return kb.at[g, rows, :] if t == 0 else vb.at[g, rows, pl.ds(0, HEAD_SIZE)]

    def kv_copy(g, t, src, dst, slot, target):
        return pltpu.make_async_remote_copy(
            src_ref=view(g, t, src),
            dst_ref=view(g, t, dst),
            send_sem=kv_send.at[g, t, slot],
            recv_sem=kv_recv.at[g, t, dst],
            device_id=target,
            device_id_type=MESH,
        )

    middle = (x == 1) | (x == 2)
    to_sib = [None] * 5
    plan = {
        0: [
            (0, x < NX - 1, 8, 6, x_up),
            (1, x == 0, 8, 2, x_dn),
            (2, None, 8, 0, nxt),
            (7, k == 0, 8, 7, sib),
        ],
        4: [
            (3, x >= 1, 0, 2, x_dn),
            (4, x == NX - 1, 0, 6, x_up),
            (7, k == 1, 0, 1, sib),
        ],
        1: [(6, middle, 6, 4, x_up), (8, None, 6, 5 + 2 * k, sib)],
        3: [(5, middle, 2, 4, x_dn), (9, None, 2, 1 + 2 * k, sib)],
        2: [(10, None, 4, 3 + 2 * k, sib)],
    }

    def kv_plan(g, t, s, act):
        for slot, cond, src, dst, target in plan[s]:
            c = kv_copy(g, t, src, dst, slot, target)
            if cond is None:
                act(c)
            else:

                @pl.when(cond)
                def _(c=c):
                    act(c)

    def kv_wait(g, t, pos):
        kv_copy(g, t, pos, pos, 0, sib).wait_recv()

    def kv_send_slot(g, t, s):
        if s:
            kv_wait(g, t, 8 - 2 * s)
        kv_plan(g, t, s, lambda c: c.start())

    def kv_rest(g):
        for t in range(2):
            for pos in (7, 5, 3, 1):
                kv_wait(g, t, pos)

    for c in kv_local:
        c.wait()
    for t in range(2):
        kv_send_slot(0, t, 0)

    for g in range(kv_heads):
        vb[g, :, pl.ds(HEAD_SIZE, HEAD_SIZE)] = jnp.ones((vb.shape[1], HEAD_SIZE), vb.dtype)
    base = i * blocks - SPAN * blocks
    lane = lax.broadcasted_iota(jnp.int32, (8, keys), 1) + first
    for j in range(blocks):
        block = base + lane // BLOCK
        keep = (block * BLOCK >= starts[j]) & (block <= i * blocks + j)
        bias[pl.ds(8 * j, 8), :] = jnp.where(keep, 0.0, MASKED)

    for t in range(2):
        for s in (4, 1):
            kv_send_slot(0, t, s)
    w_step(0)
    for t in range(2):
        for s in (3, 2):
            kv_send_slot(0, t, s)
    for t in range(2):
        kv_send_slot(1, t, 0)
    for c in q_local:
        c.wait()

    part = tok // 2

    def cols_of(n):
        return span_of(n, HEAD_SIZE)

    def h_copy(n, r):
        return pltpu.make_async_remote_copy(
            src_ref=ho.at[pl.ds(r * part, part), cols_of(n)],
            dst_ref=relay.at[r, :, cols_of(n)],
            send_sem=h_send.at[r, n],
            recv_sem=h_recv.at[r, n],
            device_id=(y_same, y_far)[r],
            device_id_type=MESH,
        )

    def f_copy(n, r):
        return pltpu.make_async_remote_copy(
            src_ref=relay.at[r, :, cols_of(n)],
            dst_ref=hin.at[pl.ds(r * part, part), cols_of(n)],
            send_sem=f_send.at[r, n],
            recv_sem=f_recv.at[r, n],
            device_id=(y_far, y_same)[r],
            device_id_type=MESH,
        )

    def forward(n):
        for r in range(2):
            h_copy(n, r).wait_recv()
            f_copy(n, r).start()

    tri = jnp.where(
        lax.broadcasted_iota(jnp.int32, (BLOCK, BLOCK), 1)
        <= lax.broadcasted_iota(jnp.int32, (BLOCK, BLOCK), 0),
        0.0,
        MASKED,
    )
    factor = HEAD_SIZE ** (-0.5) * math.log2(math.e)
    width = 2 * BLOCK
    chunks = keys // width
    own_first = SPAN * blocks - first // BLOCK

    def attend(n, g):
        q = qb[n]
        top = jnp.full((tok, BLOCK), MASKED, jnp.float32)
        for t in range(chunks):
            key = kb[g, pl.ds(first + t * width, width), :]
            s = lax.dot_general(q, key, (((1,), (1,)), ((), ())), preferred_element_type=jnp.float32)
            rows = []
            for j in range(blocks):
                lanes = []
                for u in range(2):
                    w = 2 * t + u
                    tile = s[j * BLOCK : (j + 1) * BLOCK, u * BLOCK : (u + 1) * BLOCK]
                    tile = tile + bias[pl.ds(8 * j, 1), pl.ds(w * BLOCK, BLOCK)]
                    if w == own_first + j:
                        tile = tile + tri
                    lanes.append(tile)
                rows.append(jnp.concatenate(lanes, axis=1))
            s = jnp.concatenate(rows, axis=0)
            sb[:, pl.ds(t * width, width)] = s
            top = jnp.maximum(top, jnp.maximum(s[:, :BLOCK], s[:, BLOCK:]))
        peak = jnp.max(top, axis=1, keepdims=True)
        for t in range(chunks):
            span = pl.ds(t * width, width)
            pb[:, span] = jnp.exp2((sb[:, span] - peak) * factor).astype(jnp.bfloat16)
        both = jnp.dot(pb[...], vb[g, pl.ds(first, keys), :], preferred_element_type=jnp.float32)
        out = both[:, :HEAD_SIZE] / both[:, HEAD_SIZE:]
        ho[:, cols_of(n)] = out.astype(jnp.bfloat16)
        for r in range(2):
            h_copy(n, r).start()

    tile_n = 512
    tiles = half // tile_n

    def project(src, wts, lo, hi, fresh):
        for m in range(tiles):
            cols = pl.ds(m * tile_n, tile_n)
            new = jnp.dot(src[:, lo:hi], wts[lo:hi, m * tile_n : (m + 1) * tile_n], preferred_element_type=jnp.float32)
            acc[:, cols] = new if fresh else acc[:, cols] + new

    kv_rest(0)

    def first_group(n, _):
        attend(n, 0)

        @pl.when(n == 0)
        def _():
            for t in range(2):
                for s in (4, 1):
                    kv_send_slot(1, t, s)
            w_step(1)

        @pl.when(n == 1)
        def _():
            for t in range(2):
                for s in (3, 2):
                    kv_send_slot(1, t, s)

        @pl.when(n > 0)
        def _():
            forward(n - 1)

        return 0

    lax.fori_loop(0, group, first_group, 0)
    w_step(2)
    kv_rest(1)

    def second_group(n, _):
        attend(n, 1)
        forward(n - 1)

        @pl.when(n == group + 1)
        def _():
            w_step(3)

        return 0

    lax.fori_loop(group, q_heads, second_group, 0)
    w_step(4)
    w_local.wait()
    mid = group * HEAD_SIZE
    full = q_heads * HEAD_SIZE
    forward(q_heads - 1)
    project(ho, wown, 0, full, True)
    for n in range(group):
        for r in range(2):
            f_copy(n, r).wait_recv()
    w_rest()
    project(hin, wfar, 0, mid, False)
    for n in range(group, q_heads):
        for r in range(2):
            f_copy(n, r).wait_recv()
    outs = []
    for m in range(tiles):
        cols = pl.ds(m * tile_n, tile_n)
        new = jnp.dot(hin[:, mid:], wfar[mid:, m * tile_n : (m + 1) * tile_n], preferred_element_type=jnp.float32)
        outb[:, cols] = (acc[:, cols] + new).astype(jnp.bfloat16)
        c = pltpu.make_async_copy(outb.at[:, cols], o_hbm.at[:, cols], out_sem.at[m])
        c.start()
        outs.append(c)

    w_first.wait_send()
    for d in w_plan:
        for p, sends in w_plan[d]:
            for slot, target in sends:
                w_copy(p, slot, target).wait_send()
    for g in range(kv_heads):
        for t in range(2):
            for s in plan:
                kv_plan(g, t, s, lambda c: c.wait_send())
    for n in range(q_heads):
        for r in range(2):
            h_copy(n, r).wait_send()
            f_copy(n, r).wait_send()
    for c in outs:
        c.wait()


def per_device(queries, keys, values, block_start, out_weight):
    n_ctx = lax.axis_size("ctx")
    tok = queries.shape[0]
    rows, width = out_weight.shape
    kv_heads = keys.shape[1] // HEAD_SIZE
    q_heads = queries.shape[1] // HEAD_SIZE
    half = width // 2
    nz = n_ctx // PLANE
    window = (SPAN + 1) * tok
    used = window - BLOCK
    bf16, f32 = jnp.bfloat16, jnp.float32
    dma = pltpu.SemaphoreType.DMA
    anywhere = pl.BlockSpec(memory_space=pl.ANY)
    return pl.pallas_call(
        kernel,
        out_shape=jax.ShapeDtypeStruct((tok, half), bf16),
        in_specs=[pl.BlockSpec(memory_space=pltpu.SMEM)] + [anywhere] * 4,
        out_specs=anywhere,
        scratch_shapes=[
            pltpu.VMEM((q_heads, tok, HEAD_SIZE), bf16),
            pltpu.VMEM((kv_heads, window, HEAD_SIZE), bf16),
            pltpu.VMEM((kv_heads, window, 2 * HEAD_SIZE), bf16),
            pltpu.VMEM((tok, used), f32),
            pltpu.VMEM((tok, used), bf16),
            pltpu.VMEM((8 * (tok // BLOCK), used), f32),
            pltpu.VMEM((tok, q_heads * HEAD_SIZE), bf16),
            pltpu.VMEM((tok, q_heads * HEAD_SIZE), bf16),
            pltpu.VMEM((2, tok // 2, q_heads * HEAD_SIZE), bf16),
            pltpu.VMEM((rows, half), bf16),
            pltpu.VMEM((rows, half), bf16),
            pltpu.VMEM((tok, half), f32),
            pltpu.VMEM((tok, half), bf16),
            dma((2 * kv_heads + q_heads + 1,)),
            dma((kv_heads, 2, 11)),
            dma((kv_heads, 2, SPAN + 1)),
            dma((4 * nz,)),
            dma((2 * nz,)),
            dma((2, q_heads)),
            dma((2, q_heads)),
            dma((2, q_heads)),
            dma((2, q_heads)),
            dma((half // 512,)),
        ],
        compiler_params=pltpu.CompilerParams(
            collective_id=0, has_side_effects=True, vmem_limit_bytes=56 * 1024 * 1024
        ),
    )(block_start, queries, keys, values, out_weight)


def solution(mesh):
    in_specs = (P("ctx", "head"), P("ctx", "head"), P("ctx", "head"), P("ctx"), P("head", None))
    out_specs = P("ctx", "head")
    return jax.shard_map(
        per_device, mesh=mesh, in_specs=in_specs, out_specs=out_specs, check_vma=False
    )
```

```python
import math

import jax
import jax.numpy as jnp
from jax import lax
from jax.experimental import pallas as pl
from jax.experimental.pallas import tpu as pltpu
from jax.sharding import PartitionSpec as P

HEAD_SIZE = 128
BLOCK = 128
SPAN = 8
NX = 4
NY = 2
ROW = NX * 2
PLANE = NY * ROW
MESH = pl.DeviceIdType.MESH
MASKED = -1e30


def span_of(n, size):
    start = n * size
    return pl.ds(start if isinstance(start, int) else pl.multiple_of(start, size), size)


def kernel(
    starts,
    q_hbm,
    k_hbm,
    v_hbm,
    w_hbm,
    o_hbm,
    qb,
    kb,
    vb,
    sb,
    pb,
    bias,
    ho,
    hin,
    peaks,
    wown,
    wfar,
    acc,
    outb,
    loc_sem,
    kv_send,
    kv_recv,
    w_send,
    w_recv,
    h_send,
    h_recv,
    out_sem,
):
    n_ctx = lax.axis_size("ctx")
    tok = q_hbm.shape[0]
    kv_heads = k_hbm.shape[1] // HEAD_SIZE
    q_heads = q_hbm.shape[1] // HEAD_SIZE
    group = q_heads // kv_heads
    half = outb.shape[1]
    nz = n_ctx // PLANE
    cuts = 2
    piece = wfar.shape[0] // (nz * 2 * cuts)
    up_hops = (nz - 1) // 2
    down_hops = nz - 1 - up_hops
    blocks = tok // BLOCK
    first = BLOCK
    keys = SPAN * tok + tok - first

    i = lax.axis_index("ctx")
    h = lax.axis_index("head")
    k = i % 2
    x = (i // 2) % NX
    y_lo = (i // ROW) % NY
    z = i // PLANE
    row0 = i - x * 2

    def dev(c, g):
        return {"ctx": c, "head": g}

    sib = dev(i + 1 - 2 * k, h)
    x_up = dev(row0 + ((x + 1) % NX) * 2, h)
    x_dn = dev(row0 + ((x + NX - 1) % NX) * 2, h)
    nxt = dev((i + ROW) % n_ctx, h)
    prv = dev((i + n_ctx - ROW) % n_ctx, h)
    yx = i + ROW - 2 * ROW * y_lo
    y_far = dev(yx, 1 - h)
    across = dev(i, 1 - h)
    x_two = dev(row0 + ((x + 2) % NX) * 2, h)
    z_up = dev((i + PLANE) % n_ctx, h)
    z_dn = dev((i + n_ctx - PLANE) % n_ctx, h)

    local = []

    def load(src, dst):
        c = pltpu.make_async_copy(src, dst, loc_sem.at[len(local)])
        c.start()
        local.append(c)
        return c

    own = pl.ds(SPAN * tok, tok)
    kv_local = []
    for g in range(kv_heads):
        cols = pl.ds(g * HEAD_SIZE, HEAD_SIZE)
        kv_local.append(load(k_hbm.at[:, cols], kb.at[g, own, :]))
        kv_local.append(load(v_hbm.at[:, cols], vb.at[g, own, pl.ds(0, HEAD_SIZE)]))
    q_local = [load(q_hbm.at[:, pl.ds(n * HEAD_SIZE, HEAD_SIZE)], qb.at[n]) for n in range(q_heads)]
    w_local = load(w_hbm.at[:, span_of(h, half)], wown)

    barrier = pltpu.get_barrier_semaphore()
    partners = (sib, x_up, x_dn, x_two, nxt, prv, y_far, across, z_up, z_dn)
    for d in partners:
        pl.semaphore_signal(barrier, inc=1, device_id=d, device_id_type=MESH)
    pl.semaphore_wait(barrier, len(partners))

    def w_rows(p):
        return span_of(p, piece)

    def w_copy(p, slot, target):
        return pltpu.make_async_remote_copy(
            src_ref=wfar.at[w_rows(p), :],
            dst_ref=wfar.at[w_rows(p), :],
            send_sem=w_send.at[slot],
            recv_sem=w_recv.at[p],
            device_id=target,
            device_id_type=MESH,
        )

    def w_first(c):
        p = (z * 2 + k) * cuts + c
        return pltpu.make_async_remote_copy(
            src_ref=w_hbm.at[w_rows(p), span_of(1 - h, half)],
            dst_ref=wfar.at[w_rows(p), :],
            send_sem=w_send.at[c],
            recv_sem=w_recv.at[p],
            device_id=y_far,
            device_id_type=MESH,
        )

    w_plan = {}
    slots = cuts
    for d in range(down_hops + 1):
        w_plan[d] = []
        for c in range(cuts):
            up, down = (down_hops, up_hops) if c % 2 == 0 else (up_hops, down_hops)
            routes = []
            if d == 0:
                routes.append((z, [z_up, z_dn, sib]))
            elif d <= up:
                routes.append(((z + nz - d) % nz, [z_up, sib] if d < up else [sib]))
            if 0 < d <= down:
                routes.append(((z + d) % nz, [z_dn, sib] if d < down else [sib]))
            for source, targets in routes:
                w_plan[d].append(((source * 2 + k) * cuts + c, [(slots + n, t) for n, t in enumerate(targets)]))
                slots += len(targets)

    def w_step(d):
        for p, sends in w_plan[d]:
            w_copy(p, 0, sib).wait_recv()
            for slot, target in sends:
                w_copy(p, slot, target).start()

    def w_rest():
        for other in range(nz):
            for c in range(cuts):
                w_copy((other * 2 + 1 - k) * cuts + c, 0, sib).wait_recv()

    def view(g, t, pos):
        rows = span_of(pos, tok)
        return kb.at[g, rows, :] if t == 0 else vb.at[g, rows, pl.ds(0, HEAD_SIZE)]

    def kv_copy(g, t, src, dst, slot, target):
        return pltpu.make_async_remote_copy(
            src_ref=view(g, t, src),
            dst_ref=view(g, t, dst),
            send_sem=kv_send.at[g, t, slot],
            recv_sem=kv_recv.at[g, t, dst],
            device_id=target,
            device_id_type=MESH,
        )

    plan = {
        0: [
            (0, None, 8, 0, nxt),
            (1, x <= 1, 8, 6, x_up),
            (2, x == 0, 8, 4, x_two),
            (3, x == 0, 8, 2, x_dn),
            (4, k == 0, 8, 7, sib),
        ],
        5: [(2, x == 1, 8, 4, x_two), (1, x == 2, 8, 6, x_up)],
        4: [
            (5, x >= 1, 0, 2, x_dn),
            (6, x >= 2, 0, 4, x_two),
            (7, x == NX - 1, 0, 6, x_up),
            (4, k == 1, 0, 1, sib),
        ],
        1: [(8, None, 6, 5 + 2 * k, sib)],
        3: [(9, None, 2, 1 + 2 * k, sib)],
        2: [(10, None, 4, 3 + 2 * k, sib)],
    }

    def kv_plan(g, t, s, act):
        for slot, cond, src, dst, target in plan[s]:
            c = kv_copy(g, t, src, dst, slot, target)
            if cond is None:
                act(c)
            else:

                @pl.when(cond)
                def _(c=c):
                    act(c)

    def kv_wait(g, t, pos):
        kv_copy(g, t, pos, pos, 0, sib).wait_recv()

    def kv_send_slot(g, t, s):
        if 0 < s < 5:
            kv_wait(g, t, 8 - 2 * s)
        kv_plan(g, t, s, lambda c: c.start())

    def kv_rest(g, t):
        for pos in (7, 5, 3, 1):
            kv_wait(g, t, pos)

    for c in kv_local:
        c.wait()
    for t in range(2):
        kv_send_slot(0, t, 0)
        kv_send_slot(0, t, 5)
    for c in range(cuts):
        w_first(c).start()
    for t in range(2):
        kv_send_slot(1, t, 0)

    for g in range(kv_heads):
        vb[g, :, pl.ds(HEAD_SIZE, HEAD_SIZE)] = jnp.ones((vb.shape[1], HEAD_SIZE), vb.dtype)
    base = i * blocks - SPAN * blocks
    lane = lax.broadcasted_iota(jnp.int32, (8, keys), 1) + first
    for j in range(blocks):
        block = base + lane // BLOCK
        keep = (block * BLOCK >= starts[j]) & (block <= i * blocks + j)
        bias[pl.ds(8 * j, 8), :] = jnp.where(keep, 0.0, MASKED)

    for t in range(2):
        kv_send_slot(0, t, 4)
    for t in range(2):
        kv_send_slot(1, t, 5)
    w_step(0)
    for t in range(2):
        kv_send_slot(1, t, 4)
    for n in (1, 3, 2):
        kv_send_slot(0, 0, n)
    for c in q_local:
        c.wait()

    def cols_of(n):
        return span_of(n, HEAD_SIZE)

    def h_copy(n):
        return pltpu.make_async_remote_copy(
            src_ref=ho.at[:, cols_of(n)],
            dst_ref=hin.at[:, cols_of(n)],
            send_sem=h_send.at[n],
            recv_sem=h_recv.at[n],
            device_id=across,
            device_id_type=MESH,
        )

    tri = jnp.where(
        lax.broadcasted_iota(jnp.int32, (BLOCK, BLOCK), 1)
        <= lax.broadcasted_iota(jnp.int32, (BLOCK, BLOCK), 0),
        0.0,
        MASKED,
    )
    factor = HEAD_SIZE ** (-0.5) * math.log2(math.e)
    width = 2 * BLOCK
    chunks = keys // width
    own_first = SPAN * blocks - first // BLOCK

    def score(n, g):
        q = qb[g * group + n]
        top = jnp.full((tok, BLOCK), MASKED, jnp.float32)
        for t in range(chunks):
            key = kb[g, pl.ds(first + t * width, width), :]
            s = lax.dot_general(q, key, (((1,), (1,)), ((), ())), preferred_element_type=jnp.float32)
            rows = []
            for j in range(blocks):
                lanes = []
                for u in range(2):
                    w = 2 * t + u
                    tile = s[j * BLOCK : (j + 1) * BLOCK, u * BLOCK : (u + 1) * BLOCK]
                    tile = tile + bias[pl.ds(8 * j, 1), pl.ds(w * BLOCK, BLOCK)]
                    if w == own_first + j:
                        tile = tile + tri
                    lanes.append(tile)
                rows.append(jnp.concatenate(lanes, axis=1))
            s = jnp.concatenate(rows, axis=0)
            sb[n, :, pl.ds(t * width, width)] = s
            top = jnp.maximum(top, jnp.maximum(s[:, :BLOCK], s[:, BLOCK:]))
        peaks[n] = top

    def weigh(n, g):
        peak = jnp.max(peaks[n], axis=1, keepdims=True)
        for t in range(chunks):
            span = pl.ds(t * width, width)
            pb[:, span] = jnp.exp2((sb[n, :, span] - peak) * factor).astype(jnp.bfloat16)
        both = jnp.dot(pb[...], vb[g, pl.ds(first, keys), :], preferred_element_type=jnp.float32)
        out = both[:, :HEAD_SIZE] / both[:, HEAD_SIZE:]
        ho[:, cols_of(g * group + n)] = out.astype(jnp.bfloat16)
        h_copy(g * group + n).start()

    tile_n = 512
    tiles = half // tile_n

    def project(src, wts, lo, hi, fresh):
        for m in range(tiles):
            cols = pl.ds(m * tile_n, tile_n)
            new = jnp.dot(src[:, lo:hi], wts[lo:hi, m * tile_n : (m + 1) * tile_n], preferred_element_type=jnp.float32)
            acc[:, cols] = new if fresh else acc[:, cols] + new

    kv_rest(0, 0)

    def hooks(g, n, table):
        for (at_g, at_n), acts in table.items():

            @pl.when((g == at_g) & (n == at_n))
            def _(acts=acts):
                for act in acts:
                    act()

    def slot(g, t, s):
        return lambda: kv_send_slot(g, t, s)

    after_score = {
        (0, 1): [slot(0, 1, 1)],
        (0, 2): [slot(0, 1, 3), lambda: w_step(1)],
        (0, 3): [slot(0, 1, 2), lambda: kv_rest(0, 1)],
        (1, 1): [slot(1, 1, 1)],
        (1, 2): [slot(1, 1, 3)],
        (1, 3): [slot(1, 1, 2), lambda: kv_rest(1, 1)],
    }
    after_weigh = {
        (0, 1): [slot(1, 0, 1)],
        (0, 2): [slot(1, 0, 3)],
        (0, 3): [slot(1, 0, 2), lambda: w_step(2), lambda: kv_rest(1, 0)],
        (1, 1): [lambda: w_step(3)],
    }

    def one_group(g, _):
        def one_score(n, _):
            score(n, g)
            hooks(g, n, after_score)
            return 0

        def one_weigh(n, _):
            weigh(n, g)
            hooks(g, n, after_weigh)
            return 0

        lax.fori_loop(0, group, one_score, 0)
        lax.fori_loop(0, group, one_weigh, 0)
        return 0

    lax.fori_loop(0, kv_heads, one_group, 0)
    w_local.wait()
    mid = group * HEAD_SIZE
    late = (q_heads - 2) * HEAD_SIZE
    full = q_heads * HEAD_SIZE
    project(ho, wown, 0, full, True)
    w_step(4)

    def arrive(lo, hi):
        for n in range(lo, hi):
            h_copy(n).wait_recv()

    w_rest()
    arrive(0, group)
    project(hin, wfar, 0, mid, False)
    arrive(group, q_heads - 2)
    project(hin, wfar, mid, late, False)
    arrive(q_heads - 2, q_heads)
    outs = []
    for m in range(tiles):
        cols = pl.ds(m * tile_n, tile_n)
        new = jnp.dot(hin[:, late:], wfar[late:, m * tile_n : (m + 1) * tile_n], preferred_element_type=jnp.float32)
        outb[:, cols] = (acc[:, cols] + new).astype(jnp.bfloat16)
        c = pltpu.make_async_copy(outb.at[:, cols], o_hbm.at[:, cols], out_sem.at[m])
        c.start()
        outs.append(c)

    for c in range(cuts):
        w_first(c).wait_send()
    for d in w_plan:
        for p, sends in w_plan[d]:
            for slot, target in sends:
                w_copy(p, slot, target).wait_send()
    for g in range(kv_heads):
        for t in range(2):
            for s in plan:
                kv_plan(g, t, s, lambda c: c.wait_send())
    for n in range(q_heads):
        h_copy(n).wait_send()
    for c in outs:
        c.wait()


def per_device(queries, keys, values, block_start, out_weight):
    n_ctx = lax.axis_size("ctx")
    tok = queries.shape[0]
    rows, width = out_weight.shape
    kv_heads = keys.shape[1] // HEAD_SIZE
    q_heads = queries.shape[1] // HEAD_SIZE
    half = width // 2
    nz = n_ctx // PLANE
    window = (SPAN + 1) * tok
    used = window - BLOCK
    bf16, f32 = jnp.bfloat16, jnp.float32
    dma = pltpu.SemaphoreType.DMA
    anywhere = pl.BlockSpec(memory_space=pl.ANY)
    return pl.pallas_call(
        kernel,
        out_shape=jax.ShapeDtypeStruct((tok, half), bf16),
        in_specs=[pl.BlockSpec(memory_space=pltpu.SMEM)] + [anywhere] * 4,
        out_specs=anywhere,
        scratch_shapes=[
            pltpu.VMEM((q_heads, tok, HEAD_SIZE), bf16),
            pltpu.VMEM((kv_heads, window, HEAD_SIZE), bf16),
            pltpu.VMEM((kv_heads, window, 2 * HEAD_SIZE), bf16),
            pltpu.VMEM((q_heads // kv_heads, tok, used), f32),
            pltpu.VMEM((tok, used), bf16),
            pltpu.VMEM((8 * (tok // BLOCK), used), f32),
            pltpu.VMEM((tok, q_heads * HEAD_SIZE), bf16),
            pltpu.VMEM((tok, q_heads * HEAD_SIZE), bf16),
            pltpu.VMEM((q_heads // kv_heads, tok, HEAD_SIZE), f32),
            pltpu.VMEM((rows, half), bf16),
            pltpu.VMEM((rows, half), bf16),
            pltpu.VMEM((tok, half), f32),
            pltpu.VMEM((tok, half), bf16),
            dma((2 * kv_heads + q_heads + 1,)),
            dma((kv_heads, 2, 11)),
            dma((kv_heads, 2, SPAN + 1)),
            dma((8 * nz,)),
            dma((4 * nz,)),
            dma((q_heads,)),
            dma((q_heads,)),
            dma((half // 512,)),
        ],
        compiler_params=pltpu.CompilerParams(
            collective_id=0, has_side_effects=True, vmem_limit_bytes=56 * 1024 * 1024
        ),
    )(block_start, queries, keys, values, out_weight)


def solution(mesh):
    in_specs = (P("ctx", "head"), P("ctx", "head"), P("ctx", "head"), P("ctx"), P("head", None))
    out_specs = P("ctx", "head")
    return jax.shard_map(
        per_device, mesh=mesh, in_specs=in_specs, out_specs=out_specs, check_vma=False
    )
```
